128 devices in a mesh: blk: 8 (over z_lo, x), head: 16 (over y, z_hi, core).
Axes of the slice: x: 4, y: 4, z: 4 (z_hi: 2, z_lo: 2; z = z_hi * 2 + z_lo), core: 2. Of those that a mesh axis runs over, the one named last changes fastest.
Arguments:
- qkv: bfloat16 [32768, 6144], P(('blk', 'head')), may hold values from -12 to 12
Outputs:
- attended: bfloat16 [32768, 2048], P(('blk', 'head'))
The draws below stay inside these ranges and needn't reach their ends.
All inputs are finite; a program needn't handle non-finite values.
Results may differ from the reference program's by a relative error of at most 0.0059.
Values may be sent and summed in bfloat16 or wider, within the bound.
A program may use at most 128 MiB of HBM per device.

```python
import jax
import jax.numpy as jnp
from jax import lax

HEADS = 32
HEAD_DIM = 64
BLOCK = 2048
D = 2048
TOKENS = 32768


def draw_qkv(key, part):
    first = jax.random.fold_in(key, 0)
    base = jnp.clip(jax.random.normal(first, (TOKENS, 3 * D), jnp.float32), -6.0, 6.0)
    return base.astype(jnp.bfloat16)


def setup_inputs(seed: int = 0) -> dict:
    arg_keys = jax.random.split(jax.random.key(seed), 2)
    return {
        "qkv": draw_qkv(jax.random.fold_in(arg_keys[1], 71), 0),
    }


def one_head(parts):
    nblk = TOKENS // BLOCK
    steps = nblk.bit_length() - 1
    scale = HEAD_DIM ** -0.5
    results = []
    for block_a in range(nblk):
        query = parts[0, block_a]
        partners = [block_a] + [block_a ^ (1 << i) for i in range(steps)]
        maxima, totals, values = [], [], []
        for block_c in partners:
            scores = jnp.dot(query, parts[1, block_c].T, preferred_element_type=jnp.float32) * scale
            row_max = jnp.max(scores, axis=1, keepdims=True)
            probs = jnp.exp(scores - row_max).astype(jnp.bfloat16)
            totals.append(jnp.sum(probs.astype(jnp.float32), axis=1, keepdims=True))
            values.append(jnp.dot(probs, parts[2, block_c], preferred_element_type=jnp.float32))
            maxima.append(row_max)
        overall = maxima[0]
        for row_max in maxima[1:]:
            overall = jnp.maximum(overall, row_max)
        numer = jnp.zeros_like(values[0])
        denom = jnp.zeros_like(totals[0])
        for row_max, total, value in zip(maxima, totals, values):
            factor = jnp.exp(row_max - overall)
            numer = numer + factor * value
            denom = denom + factor * total
        results.append(numer / denom)
    return jnp.stack(results)


def reference(qkv):
    nblk = TOKENS // BLOCK
    grid = qkv.reshape(nblk, BLOCK, 3, HEADS, HEAD_DIM).transpose(3, 2, 0, 1, 4)
    result = lax.map(one_head, grid)
    return result.transpose(1, 2, 0, 3).reshape(TOKENS, D).astype(jnp.bfloat16)
```

```python
import math

import jax
import jax.numpy as jnp
from jax import lax
from jax.experimental import pallas as pl
from jax.experimental.pallas import tpu as pltpu
from jax.sharding import PartitionSpec as P

HEAD_DIM = 64
BLOCK = 2048
NBLK = 16
HEADS = 32
D = HEADS * HEAD_DIM
CHIPS = 64
ROWS = 256
PART = 64
QT = 512
KC = 512
PAIRS = 5 * NBLK
SCALE = HEAD_DIM ** -0.5 * math.log2(math.e)
MESH_ID = pl.DeviceIdType.MESH


def xor(a, b, bits):
    total = 0
    for i in range(bits):
        w = 1 << i
        total = total + w * lax.rem(lax.rem(lax.div(a, w), 2) + lax.rem(lax.div(b, w), 2), 2)
    return total


def pair_of(n):
    c = lax.div(n, 5)
    i = lax.rem(n, 5)
    w = jnp.where(i == 4, 0, jnp.where(i == 0, 1, jnp.where(i == 1, 2, jnp.where(i == 2, 4, 8))))
    return xor(c, w, 4), c


def kernel(
    x_ref, out_ref,
    sendq, sendkv, qb, kvb, qs, kk, va, m_ref, acc, s0, s1, al0, al1, mn0, mn1, osend, obuf,
    q_send, q_recv, kv_send, kv_recv, f_send, f_recv, o_send, o_recv, loc,
):
    blk = lax.axis_index("blk")
    head = lax.axis_index("head")
    chip = blk * 8 + lax.div(head, 2)
    core = lax.rem(head, 2)
    f32, bf16 = jnp.float32, jnp.bfloat16

    def dev(c):
        return (lax.div(c, 8), lax.rem(c, 8) * 2 + core)

    sibling = (blk, head + 1 - 2 * core)

    barrier = pltpu.get_barrier_semaphore()

    @pl.loop(1, CHIPS)
    def _(t):
        pl.semaphore_signal(barrier, inc=1, device_id=dev(xor(chip, t, 6)), device_id_type=MESH_ID)

    pl.semaphore_signal(barrier, inc=1, device_id=sibling, device_id_type=MESH_ID)

    @pl.loop(0, HEADS // 2)
    def _(g):
        x = x_ref[:, pl.ds(pl.multiple_of(g * 128, 128), 128)]
        for e in range(2):
            y = x[:, e * 64:(e + 1) * 64]
            for c in range(2):
                sendq[g * 4 + e * 2 + c] = jnp.concatenate(
                    [y[c * 128:c * 128 + 64], y[c * 128 + 64:c * 128 + 128]], axis=1
                )

    pl.semaphore_wait(barrier, CHIPS)

    @pl.loop(1, CHIPS)
    def _(t):
        to = xor(chip, t, 6)
        pltpu.make_async_remote_copy(
            sendq.at[to], qb.at[t], q_send, q_recv, device_id=dev(to), device_id_type=MESH_ID
        ).start()

    @pl.loop(0, HEADS // 2)
    def _(g):
        k = x_ref[:, pl.ds(pl.multiple_of(D + g * 128, 128), 128)]
        v = x_ref[:, pl.ds(pl.multiple_of(2 * D + g * 128, 128), 128)]
        for e in range(2):
            h = slice(e * 64, (e + 1) * 64)
            sendkv[g * 2 + e] = jnp.concatenate([k[:, h], v[:, h]], axis=1)

    @pl.loop(1, CHIPS)
    def _(t):
        to = xor(chip, t, 6)
        pltpu.make_async_remote_copy(
            sendkv.at[lax.div(to, 2)], kvb.at[core, t], kv_send, kv_recv.at[lax.div(t, 4)],
            device_id=dev(to), device_id_type=MESH_ID,
        ).start()

    own_q = pltpu.make_async_copy(sendq.at[chip], qb.at[0], loc.at[0])
    own_kv = pltpu.make_async_copy(sendkv.at[lax.div(chip, 2)], kvb.at[core, 0], loc.at[1])
    own_q.start()
    own_kv.start()

    def forward(c):
        rows = pl.ds(c * 4, 4)
        return pltpu.make_async_remote_copy(
            kvb.at[core, rows], kvb.at[core, rows], f_send, f_recv.at[c],
            device_id=sibling, device_id_type=MESH_ID,
        )

    def landed(c, skip):
        part = kvb.at[core, pl.ds(c * 4 + skip, 4 - skip)]
        pltpu.make_async_remote_copy(
            part, part, kv_send, kv_recv.at[c], device_id=sibling, device_id_type=MESH_ID
        ).wait_recv()

    def arrive(c):
        landed(c, 0)
        forward(c).start()

    def ready(c):
        part = kvb.at[1 - core, pl.ds(c * 4, 4)]
        pltpu.make_async_remote_copy(
            part, part, f_send, f_recv.at[c], device_id=sibling, device_id_type=MESH_ID
        ).wait_recv()
        slot = lax.rem(c, 2)
        low = lax.broadcasted_iota(jnp.int32, (ROWS, 128), 1) < 64

        @pl.loop(0, 2)
        def _(z):
            @pl.loop(0, 4)
            def _(w):
                t = kvb[z, c * 4 + w]
                rows = pl.ds(pl.multiple_of((z * 4 + w) * ROWS, ROWS), ROWS)
                kk[slot, rows] = jnp.concatenate([t[:, :64], t[:, :64]], axis=1)
                va[slot, rows] = jnp.where(low, jnp.ones_like(t), t)

    own_kv.wait()
    landed(0, 1)
    forward(0).start()

    m_ref[...] = jnp.full_like(m_ref, -jnp.inf)
    acc[...] = jnp.zeros_like(acc)

    own_q.wait()
    qall = qb.at[pl.ds(1, CHIPS - 1)]
    pltpu.make_async_remote_copy(
        qall, qall, q_send, q_recv, device_id=sibling, device_id_type=MESH_ID
    ).wait_recv()

    @pl.loop(0, NBLK)
    def _(a):
        x = qb[pl.ds(a * 4, 4)].reshape(ROWS, 128).astype(f32) * SCALE
        hi = x.astype(bf16)
        lo = (x - hi.astype(f32)).astype(bf16)
        qs[a, 0:ROWS] = jnp.concatenate([hi[:, :64], lo[:, :64]], axis=1)
        qs[a, ROWS:QT] = jnp.concatenate([hi[:, 64:], lo[:, 64:]], axis=1)

    def stage(na, nb, sa, sb, ala, alb, mna, mnb):
        if na is not None:
            a, c = pair_of(na)
            kslot = lax.rem(c, 2)
            q = qs[a]
            m_old = m_ref[a]
            mx = None
        if nb is not None:
            a2, c2 = pair_of(nb)
            vslot = lax.rem(c2, 2)
            m_b = mnb[...]
            o = None
        for j in range(BLOCK // KC):
            ks = slice(j * KC, (j + 1) * KC)
            if na is not None:
                s = lax.dot_general(
                    q, kk[kslot, ks], (((1,), (1,)), ((), ())), preferred_element_type=f32
                )
                sa[:, ks] = s
                for l in range(KC // 128):
                    t = s[:, l * 128:(l + 1) * 128]
                    mx = t if mx is None else jnp.maximum(mx, t)
            if nb is not None:
                ps = []
                for l in range(KC // 128):
                    at = j * KC + l * 128
                    ps.append(jnp.exp2(sb[:, at:at + 128] - m_b).astype(bf16))
                p = jnp.concatenate(ps, axis=1)
                part = jnp.dot(p, va[vslot, ks], preferred_element_type=f32)
                o = part if o is None else o + part
        if nb is not None:
            acc[a2] = acc[a2] * alb[...] + o
        if na is not None:
            m_new = jnp.maximum(m_old, jnp.max(mx, axis=1, keepdims=True))
            m_ref[a] = m_new
            mna[...] = m_new
            ala[...] = jnp.exp2(m_old - m_new)

    def before(n):
        c = lax.div(n, 5)
        i = lax.rem(n, 5)

        @pl.when(jnp.logical_and(i == 2, c < NBLK - 1))
        def _():
            arrive(c + 1)

        @pl.when(jnp.logical_and(i == 0, n < PAIRS))
        def _():
            ready(c)

    def finish(n):
        a, c = pair_of(n)
        i = lax.rem(n, 5)
        last = (jnp.logical_and(i == 4, c == 15))
        for b in range(4):
            last = jnp.logical_or(last, jnp.logical_and(i == b, lax.div(c, 1 << b) == (16 >> b) - 1))

        @pl.when(last)
        def _():
            y = acc[a]
            y = y / y[:, :1]
            y = y.astype(bf16)
            z = jnp.concatenate([y[:ROWS, 64:], y[ROWS:, 64:]], axis=1)
            osend[pl.ds(a * 4, 4)] = z.reshape(4, PART, 128)

            @pl.loop(0, 4)
            def _(w):
                t = a * 4 + w
                to = xor(chip, t, 6)

                @pl.when(t > 0)
                def _():
                    pltpu.make_async_remote_copy(
                        osend.at[t], obuf.at[chip], o_send, o_recv,
                        device_id=dev(to), device_id_type=MESH_ID,
                    ).start()

                @pl.when(t == 0)
                def _():
                    own = pltpu.make_async_copy(osend.at[t], obuf.at[chip], loc.at[2])
                    own.start()
                    own.wait()

    ready(0)
    stage(0, None, s0, s1, al0, al1, mn0, mn1)

    @pl.loop(0, PAIRS // 2)
    def _(h):
        n = h * 2
        before(n + 1)
        stage(n + 1, n, s1, s0, al1, al0, mn1, mn0)
        before(n + 2)
        stage(jnp.minimum(n + 2, PAIRS - 1), n + 1, s0, s1, al0, al1, mn0, mn1)

        @pl.loop(0, 2)
        def _(u):
            finish(n + u)

    def done(ref, sem):
        return pltpu.make_async_remote_copy(
            ref, ref, sem, sem, device_id=sibling, device_id_type=MESH_ID
        )

    done(obuf.at[pl.ds(0, CHIPS - 1)], o_recv).wait_recv()

    @pl.loop(0, HEADS // 2)
    def _(g):
        cols = pl.ds(pl.multiple_of(g * 128, 128), 128)
        for c in range(2):
            e = obuf[g * 4 + c]
            o = obuf[g * 4 + 2 + c]
            out_ref[c * 128:c * 128 + 64, cols] = jnp.concatenate([e[:, :64], o[:, :64]], axis=1)
            out_ref[c * 128 + 64:c * 128 + 128, cols] = jnp.concatenate(
                [e[:, 64:], o[:, 64:]], axis=1
            )

    done(osend.at[pl.ds(0, CHIPS - 1)], o_send).wait_send()
    done(qb.at[pl.ds(0, CHIPS - 1)], q_send).wait_send()
    done(kvb.at[0, pl.ds(0, CHIPS - 1)], kv_send).wait_send()
    done(kvb.at[0], f_send).wait_send()


def on_device(qkv):
    vmem = pltpu.VMEM
    bf16, f32 = jnp.bfloat16, jnp.float32
    dma = pltpu.SemaphoreType.DMA
    return pl.pallas_call(
        kernel,
        name="butterfly",
        out_shape=jax.ShapeDtypeStruct((ROWS, D), bf16),
        in_specs=[pl.BlockSpec(memory_space=vmem)],
        out_specs=pl.BlockSpec(memory_space=vmem),
        scratch_shapes=[
            vmem((CHIPS, PART, 128), bf16),
            vmem((HEADS, ROWS, 128), bf16),
            vmem((CHIPS, PART, 128), bf16),
            vmem((2, CHIPS, ROWS, 128), bf16),
            vmem((NBLK, QT, 128), bf16),
            vmem((2, BLOCK, 128), bf16),
            vmem((2, BLOCK, 128), bf16),
            vmem((NBLK, QT, 128), f32),
            vmem((NBLK, QT, 128), f32),
            vmem((QT, BLOCK), f32),
            vmem((QT, BLOCK), f32),
            vmem((QT, 128), f32),
            vmem((QT, 128), f32),
            vmem((QT, 128), f32),
            vmem((QT, 128), f32),
            vmem((CHIPS, PART, 128), bf16),
            vmem((CHIPS, PART, 128), bf16),
            dma, dma, dma, dma((NBLK,)), dma, dma((NBLK,)), dma, dma, dma((3,)),
        ],
        compiler_params=pltpu.CompilerParams(
            collective_id=0, has_side_effects=True, vmem_limit_bytes=60 * 2**20
        ),
    )(qkv)


def solution(mesh):
    spec = P(("blk", "head"), None)
    return jax.shard_map(
        on_device, mesh=mesh, in_specs=(spec,), out_specs=spec, check_vma=False
    )
```

```python
import math

import jax
import jax.numpy as jnp
from jax import lax
from jax.experimental import pallas as pl
from jax.experimental.pallas import tpu as pltpu
from jax.sharding import PartitionSpec as P

HEAD_DIM = 64
BLOCK = 2048
NBLK = 16
HEADS = 32
D = HEADS * HEAD_DIM
CHIPS = 64
ROWS = 256
PART = 64
QT = 512
KC = 512
PAIRS = 5 * NBLK
SCALE = HEAD_DIM**-0.5 * math.log2(math.e)
MESH_ID = pl.DeviceIdType.MESH


def over_bits(count, body):
    def level(bits):
        if len(bits) == count:
            body(*bits)
            return

        @pl.loop(0, 2)
        def _(b):
            level(bits + (b,))

    level(())


def kernel(
    x_ref, out_ref,
    sendq, sendkv, qb, kvb, qs, va, m_ref, acc, s0, s1, al0, al1, mn0, mn1, osend, obuf,
    q_send, q_recv, kv_send, kv_recv, f_send, f_recv, o_send, o_recv, loc,
):
    blk = lax.axis_index("blk")
    head = lax.axis_index("head")
    chip = blk * 8 + lax.div(head, 2)
    core = lax.rem(head, 2)
    f32, bf16 = jnp.float32, jnp.bfloat16

    flip = []
    for i in range(6):
        w = 32 >> i
        flip.append(w * (1 - 2 * lax.rem(lax.div(chip, w), 2)))
    sibling = (blk, head + 1 - 2 * core)

    def every_chip(body):
        def four(b5, b4, b3, b2):
            r = 8 * b5 + 4 * b4 + 2 * b3 + b2
            high = b5 * flip[0] + b4 * flip[1] + b3 * flip[2]
            to_blk = blk + lax.div(high, 8)
            for w in range(4):
                mid = b2 * flip[3] + (w // 2) * flip[4]
                low = mid + (w % 2) * flip[5]
                to = chip + high + low
                owned = half + lax.div(high + mid, 2)
                device = (to_blk, head + 2 * low)
                if w:
                    body(r * 4 + w, to, owned, device)
                else:

                    @pl.when(r > 0)
                    def _():
                        body(r * 4, to, owned, device)

        over_bits(4, four)

    half = lax.div(chip, 2)
    barrier = pltpu.get_barrier_semaphore()

    @every_chip
    def _(t, to, owned, device):
        pl.semaphore_signal(barrier, inc=1, device_id=device, device_id_type=MESH_ID)

    pl.semaphore_signal(barrier, inc=1, device_id=sibling, device_id_type=MESH_ID)

    @pl.loop(0, HEADS // 2)
    def _(g):
        x = x_ref[:, pl.ds(pl.multiple_of(g * 128, 128), 128)]
        for e in range(2):
            y = x[:, e * 64:(e + 1) * 64]
            for c in range(2):
                sendq[g * 4 + e * 2 + c] = jnp.concatenate(
                    [y[c * 128:c * 128 + 64], y[c * 128 + 64:c * 128 + 128]], axis=1
                )

    @pl.loop(0, HEADS // 2)
    def _(g):
        k = x_ref[:, pl.ds(pl.multiple_of(D + g * 128, 128), 128)]
        v = x_ref[:, pl.ds(pl.multiple_of(2 * D + g * 128, 128), 128)]
        for e in range(2):
            h = slice(e * 64, (e + 1) * 64)
            sendkv[g * 2 + e] = jnp.concatenate([k[:, h], v[:, h]], axis=1)

    pl.semaphore_wait(barrier, CHIPS)

    def place(b3, b2, b1, b0, w):
        high = b3 * flip[0] + b2 * flip[1] + b1 * flip[2]
        mid = b0 * flip[3] + (w // 2) * flip[4]
        low = mid + (w % 2) * flip[5]
        return chip + high + low, half + lax.div(high + mid, 2), (blk + lax.div(high, 8), head + 2 * low)

    def bits_of(r):
        return [lax.div(r, 8 >> i) - 2 * lax.div(r, 16 >> i) for i in range(4)]

    def send_q(r):
        for w in range(4):
            if r == 0 and w == 0:
                continue
            to, _, device = place(*[(r >> (3 - i)) & 1 for i in range(4)], w)
            pltpu.make_async_remote_copy(
                sendq.at[to], qb.at[r * 4 + w], q_send, q_recv.at[r],
                device_id=device, device_id_type=MESH_ID,
            ).start()

    def send_kv(r):
        static = isinstance(r, int)
        bits = [(r >> (3 - i)) & 1 for i in range(4)] if static else bits_of(r)
        for w in range(4):
            if static and r == 0 and w == 0:
                continue
            _, owned, device = place(*bits, w)
            pltpu.make_async_remote_copy(
                sendkv.at[owned], kvb.at[core, r * 4 + w], kv_send, kv_recv.at[r],
                device_id=device, device_id_type=MESH_ID,
            ).start()

    for r in (0, 1, 2, 4, 8):
        send_q(r)
    send_kv(0)
    for r in (3, 5, 9):
        send_q(r)
    send_kv(1)

    own_q = pltpu.make_async_copy(sendq.at[chip], qb.at[0], loc.at[0])
    own_kv = pltpu.make_async_copy(sendkv.at[half], kvb.at[core, 0], loc.at[1])
    own_q.start()
    own_kv.start()

    def forward(c):
        rows = pl.ds(c * 4, 4)
        return pltpu.make_async_remote_copy(
            kvb.at[core, rows], kvb.at[core, rows], f_send, f_recv.at[c],
            device_id=sibling, device_id_type=MESH_ID,
        )

    def landed(c, skip):
        part = kvb.at[core, pl.ds(c * 4 + skip, 4 - skip)]
        pltpu.make_async_remote_copy(
            part, part, kv_send, kv_recv.at[c], device_id=sibling, device_id_type=MESH_ID
        ).wait_recv()

    def arrive(c):
        landed(c, 0)
        forward(c).start()

    def ready(c, slot):
        part = kvb.at[1 - core, pl.ds(c * 4, 4)]
        pltpu.make_async_remote_copy(
            part, part, f_send, f_recv.at[c], device_id=sibling, device_id_type=MESH_ID
        ).wait_recv()
        low = lax.broadcasted_iota(jnp.int32, (ROWS, 128), 1) < 64

        @pl.loop(0, 2)
        def _(z):
            for w in range(4):
                t = kvb[z, c * 4 + w]
                rows = pl.ds(pl.multiple_of((z * 4 + w) * ROWS, ROWS), ROWS)
                va[slot, rows] = jnp.where(low, jnp.ones_like(t), t)

    own_kv.wait()
    landed(0, 1)
    forward(0).start()

    m_ref[...] = jnp.full_like(m_ref, -jnp.inf)
    acc[...] = jnp.zeros_like(acc)

    own_q.wait()
    def queries(a, own=0):
        got = qb.at[pl.ds(a * 4 + own, 4 - own)]
        pltpu.make_async_remote_copy(
            got, got, q_send, q_recv.at[a], device_id=sibling, device_id_type=MESH_ID
        ).wait_recv()
        x = qb[pl.ds(a * 4, 4)].reshape(ROWS, 128)
        zero = jnp.zeros((ROWS, 64), bf16)
        qs[a, 0:ROWS] = jnp.concatenate([x[:, :64], zero], axis=1)
        qs[a, ROWS:QT] = jnp.concatenate([x[:, 64:], zero], axis=1)

    queries(0, 1)

    def stage(na, nb, sa, sb, ala, alb, mna, mnb):
        if na is not None:
            a, c, _ = na
            q = qs[a]
            m_old = m_ref[a]
            mx = None
        if nb is not None:
            a2, _, vslot = nb
            m_b = mnb[...]
            o = None
        for j in range(BLOCK // KC):
            ks = slice(j * KC, (j + 1) * KC)
            if na is not None:
                s = lax.dot_general(
                    q,
                    kvb[j // 2, pl.ds(c * 4 + 2 * (j % 2), 2)].reshape(KC, 128),
                    (((1,), (1,)), ((), ())),
                    preferred_element_type=f32,
                )
                sa[:, ks] = s
                for l in range(KC // 128):
                    t = s[:, l * 128:(l + 1) * 128]
                    mx = t if mx is None else jnp.maximum(mx, t)
            if nb is not None:
                ps = []
                for l in range(KC // 128):
                    at = j * KC + l * 128
                    ps.append(jnp.exp2((sb[:, at:at + 128] - m_b) * SCALE).astype(bf16))
                p = jnp.concatenate(ps, axis=1)
                part = jnp.dot(p, va[vslot, ks], preferred_element_type=f32)
                o = part if o is None else o + part
        if nb is not None:
            acc[a2] = acc[a2] * alb[...] + o
        if na is not None:
            m_new = jnp.maximum(m_old, jnp.max(mx, axis=1, keepdims=True))
            m_ref[a] = m_new
            mna[...] = m_new
            ala[...] = jnp.exp2((m_old - m_new) * SCALE)

    def finish(a, last):
        @pl.when(last)
        def _():
            y = acc[a]
            total = jnp.concatenate([y[:ROWS, :64], y[ROWS:, :64]], axis=1)
            z = jnp.concatenate([y[:ROWS, 64:], y[ROWS:, 64:]], axis=1)
            z = (z / total).astype(bf16)
            osend[pl.ds(a * 4, 4)] = z.reshape(4, PART, 128)
            b3 = lax.div(a, 8)
            b2 = lax.div(a, 4) - 2 * b3
            b1 = lax.div(a, 2) - 4 * b3 - 2 * b2
            b0 = a - 8 * b3 - 4 * b2 - 2 * b1
            high = b3 * flip[0] + b2 * flip[1] + b1 * flip[2]
            for w in range(4):
                low = b0 * flip[3] + (w // 2) * flip[4] + (w % 2) * flip[5]

                def send():
                    pltpu.make_async_remote_copy(
                        osend.at[a * 4 + w], obuf.at[chip], o_send, o_recv,
                        device_id=(blk + lax.div(high, 8), head + 2 * low), device_id_type=MESH_ID,
                    ).start()

                if w:
                    send()
                else:
                    pl.when(a > 0)(send)

                    @pl.when(a == 0)
                    def _():
                        own = pltpu.make_async_copy(osend.at[0], obuf.at[chip], loc.at[2])
                        own.start()
                        own.wait()

    even, odd = (s0, al0, mn0), (s1, al1, mn1)

    def step(na, nb, turn):
        x, y = (odd, even) if turn else (even, odd)
        stage(na, nb, x[0], y[0], x[1], y[1], x[2], y[2])

    ready(0, 0)
    queries(1)
    step((1, 0, 0), None, 0)

    def two_blocks(b3, b2, b1):
        h = 4 * b3 + 2 * b2 + b1
        more = h < NBLK // 2 - 1
        pairs, lasts, news = [], [], []
        for b0 in range(2):
            c = 2 * h + b0
            ones = [b3 * b2 * b1 * b0, b3 * b2 * b1, b3 * b2, b3, b3 * b2 * b1 * b0]
            fresh = [b3 + b2 + b1 == 0, b3 + b2 + b1 == 0, b3 + b2 == 0, b3 == 0]
            near = [1 - 2 * b0, 2 - 4 * b1, 4 - 8 * b2, 8 - 16 * b3, 0]
            for i in range(5):
                pairs.append((c + near[i], c, b0))
                news.append(fresh[i] if i < 4 and not (b0 and i == 0) else None)
                lasts.append(None if i in (0, 4) and b0 == 0 else ones[i] == 1)
        for k in range(10):
            if k in (0, 2, 4, 6):

                @pl.when(h < (4 if k < 4 else 3))
                def _():
                    send_kv(4 * h + 2 + k // 2)

            later_q = {1: (6, 10), 3: (7, 11), 5: (12, 13), 7: (14, 15)}.get(k, ())
            if later_q:

                @pl.when(h == 0)
                def _():
                    for r in later_q:
                        send_q(r)

            if k == 1:
                arrive(2 * h + 1)
            if k == 4:
                ready(2 * h + 1, 1)
            if k == 6:

                @pl.when(more)
                def _():
                    arrive(2 * h + 2)

            turn = (k + 1) % 2
            if k < 9:
                if news[k + 1] is not None:
                    pl.when(news[k + 1])(lambda: queries(pairs[k + 1][0]))
                step(pairs[k + 1], pairs[k], turn)
            else:

                @pl.when(more)
                def _():
                    ready(2 * h + 2, 0)
                    step((2 * h + 3, 2 * h + 2, 0), pairs[9], turn)

                @pl.when(jnp.logical_not(more))
                def _():
                    step(None, pairs[9], turn)

            if lasts[k] is not None:
                finish(pairs[k][0], lasts[k])

    over_bits(3, two_blocks)

    def done(ref, sem):
        return pltpu.make_async_remote_copy(
            ref, ref, sem, sem, device_id=sibling, device_id_type=MESH_ID
        )

    done(obuf.at[pl.ds(0, CHIPS - 1)], o_recv).wait_recv()

    @pl.loop(0, HEADS // 2)
    def _(g):
        cols = pl.ds(pl.multiple_of(g * 128, 128), 128)
        for c in range(2):
            e = obuf[g * 4 + c]
            o = obuf[g * 4 + 2 + c]
            out_ref[c * 128:c * 128 + 64, cols] = jnp.concatenate([e[:, :64], o[:, :64]], axis=1)
            out_ref[c * 128 + 64:c * 128 + 128, cols] = jnp.concatenate(
                [e[:, 64:], o[:, 64:]], axis=1
            )

    done(osend.at[pl.ds(0, CHIPS - 1)], o_send).wait_send()
    done(qb.at[pl.ds(0, CHIPS - 1)], q_send).wait_send()
    done(kvb.at[0, pl.ds(0, CHIPS - 1)], kv_send).wait_send()
    done(kvb.at[0], f_send).wait_send()


def on_device(qkv):
    vmem = pltpu.VMEM
    bf16, f32 = jnp.bfloat16, jnp.float32
    dma = pltpu.SemaphoreType.DMA
    return pl.pallas_call(
        kernel,
        name="butterfly",
        out_shape=jax.ShapeDtypeStruct((ROWS, D), bf16),
        in_specs=[pl.BlockSpec(memory_space=vmem)],
        out_specs=pl.BlockSpec(memory_space=vmem),
        scratch_shapes=[
            vmem((CHIPS, PART, 128), bf16),
            vmem((HEADS, ROWS, 128), bf16),
            vmem((CHIPS, PART, 128), bf16),
            vmem((2, CHIPS, ROWS, 128), bf16),
            vmem((NBLK, QT, 128), bf16),
            vmem((2, BLOCK, 128), bf16),
            vmem((NBLK, QT, 128), f32),
            vmem((NBLK, QT, 128), f32),
            vmem((QT, BLOCK), f32),
            vmem((QT, BLOCK), f32),
            vmem((QT, 128), f32),
            vmem((QT, 128), f32),
            vmem((QT, 128), f32),
            vmem((QT, 128), f32),
            vmem((CHIPS, PART, 128), bf16),
            vmem((CHIPS, PART, 128), bf16),
            dma, dma((NBLK,)), dma, dma((NBLK,)), dma, dma((NBLK,)), dma, dma, dma((3,)),
        ],
        compiler_params=pltpu.CompilerParams(
            collective_id=0, has_side_effects=True, vmem_limit_bytes=60 * 2**20
        ),
    )(qkv)


def solution(mesh):
    spec = P(("blk", "head"), None)
    return jax.shard_map(
        on_device, mesh=mesh, in_specs=(spec,), out_specs=spec, check_vma=False
    )
```

```python
import math

import jax
import jax.numpy as jnp
from jax import lax
from jax.experimental import pallas as pl
from jax.experimental.pallas import tpu as pltpu
from jax.sharding import PartitionSpec as P

HEAD_DIM = 64
BLOCK = 2048
NBLK = 16
HEADS = 32
D = HEADS * HEAD_DIM
CHIPS = 64
ROWS = 256
PART = 64
QT = 512
KC = 512
PAIRS = 5 * NBLK
SCALE = HEAD_DIM**-0.5 * math.log2(math.e)
MESH_ID = pl.DeviceIdType.MESH


def over_bits(count, body):
    def level(bits):
        if len(bits) == count:
            body(*bits)
            return

        @pl.loop(0, 2)
        def _(b):
            level(bits + (b,))

    level(())


def kernel(
    qkv_ref, out_ref,
    x_ref, sendq, sendkv, qb, kvb, qs, va, m_ref, acc, s0, s1, al0, al1, mn0, mn1, osend, obuf,
    q_send, q_recv, kv_send, kv_recv, f_send, f_recv, o_send, o_recv, loc,
):
    blk = lax.axis_index("blk")
    head = lax.axis_index("head")
    chip = blk * 8 + lax.div(head, 2)
    core = lax.rem(head, 2)
    f32, bf16 = jnp.float32, jnp.bfloat16

    flip = []
    for i in range(6):
        w = 32 >> i
        flip.append(w * (1 - 2 * lax.rem(lax.div(chip, w), 2)))
    sibling = (blk, head + 1 - 2 * core)

    half = lax.div(chip, 2)
    def place(b3, b2, b1, b0, w):
        high = b3 * flip[0] + b2 * flip[1] + b1 * flip[2]
        mid = b0 * flip[3] + (w // 2) * flip[4]
        low = mid + (w % 2) * flip[5]
        return chip + high + low, half + lax.div(high + mid, 2), (blk + lax.div(high, 8), head + 2 * low)

    load = pltpu.make_async_copy(qkv_ref, x_ref, loc.at[3])
    load.start()
    barrier = pltpu.get_barrier_semaphore()

    for r in range(NBLK):
        for w in range(4):
            if r + w:
                _, _, device = place(*[(r >> (3 - i)) & 1 for i in range(4)], w)
                pl.semaphore_signal(barrier, inc=1, device_id=device, device_id_type=MESH_ID)

    pl.semaphore_signal(barrier, inc=1, device_id=sibling, device_id_type=MESH_ID)

    load.wait()

    @pl.loop(0, HEADS // 2)
    def _(g):
        x = x_ref[:, pl.ds(pl.multiple_of(g * 128, 128), 128)]
        for e in range(2):
            y = x[:, e * 64:(e + 1) * 64]
            for c in range(2):
                sendq[g * 4 + e * 2 + c] = jnp.concatenate(
                    [y[c * 128:c * 128 + 64], y[c * 128 + 64:c * 128 + 128]], axis=1
                )

    @pl.loop(0, HEADS // 2)
    def _(g):
        k = x_ref[:, pl.ds(pl.multiple_of(D + g * 128, 128), 128)]
        v = x_ref[:, pl.ds(pl.multiple_of(2 * D + g * 128, 128), 128)]
        for e in range(2):
            h = slice(e * 64, (e + 1) * 64)
            sendkv[g * 2 + e] = jnp.concatenate([k[:, h], v[:, h]], axis=1)

    pl.semaphore_wait(barrier, CHIPS)

    def bits_of(r):
        return [lax.div(r, 8 >> i) - 2 * lax.div(r, 16 >> i) for i in range(4)]

    def send_q(r):
        for w in range(4):
            if r == 0 and w == 0:
                continue
            to, _, device = place(*[(r >> (3 - i)) & 1 for i in range(4)], w)
            pltpu.make_async_remote_copy(
                sendq.at[to], qb.at[r * 4 + w], q_send, q_recv.at[r],
                device_id=device, device_id_type=MESH_ID,
            ).start()

    def send_kv(r):
        static = isinstance(r, int)
        bits = [(r >> (3 - i)) & 1 for i in range(4)] if static else bits_of(r)
        for w in range(4):
            if static and r == 0 and w == 0:
                continue
            _, owned, device = place(*bits, w)
            pltpu.make_async_remote_copy(
                sendkv.at[owned], kvb.at[core, r * 4 + w], kv_send, kv_recv.at[r],
                device_id=device, device_id_type=MESH_ID,
            ).start()

    send_kv(0)
    for r in (1, 2, 4, 8, 0):
        send_q(r)
    for r in (3, 5, 9):
        send_q(r)
    send_kv(1)

    own_q = pltpu.make_async_copy(sendq.at[chip], qb.at[0], loc.at[0])
    own_kv = pltpu.make_async_copy(sendkv.at[half], kvb.at[core, 0], loc.at[1])
    own_q.start()
    own_kv.start()

    def forward(c):
        rows = pl.ds(c * 4, 4)
        return pltpu.make_async_remote_copy(
            kvb.at[core, rows], kvb.at[core, rows], f_send, f_recv.at[c],
            device_id=sibling, device_id_type=MESH_ID,
        )

    def landed(c, skip):
        part = kvb.at[core, pl.ds(c * 4 + skip, 4 - skip)]
        pltpu.make_async_remote_copy(
            part, part, kv_send, kv_recv.at[c], device_id=sibling, device_id_type=MESH_ID
        ).wait_recv()

    def arrive(c):
        landed(c, 0)
        forward(c).start()

    def ready(c, slot):
        part = kvb.at[1 - core, pl.ds(c * 4, 4)]
        pltpu.make_async_remote_copy(
            part, part, f_send, f_recv.at[c], device_id=sibling, device_id_type=MESH_ID
        ).wait_recv()
        low = lax.broadcasted_iota(jnp.int32, (ROWS, 128), 1) < 64

        @pl.loop(0, 2)
        def _(z):
            for w in range(4):
                t = kvb[z, c * 4 + w]
                rows = pl.ds(pl.multiple_of((z * 4 + w) * ROWS, ROWS), ROWS)
                va[slot, rows] = jnp.where(low, jnp.ones_like(t), t)

    own_kv.wait()
    landed(0, 1)
    forward(0).start()

    m_ref[...] = jnp.full_like(m_ref, -jnp.inf)
    acc[...] = jnp.zeros_like(acc)

    own_q.wait()
    def queries(a, own=0):
        got = qb.at[pl.ds(a * 4 + own, 4 - own)]
        pltpu.make_async_remote_copy(
            got, got, q_send, q_recv.at[a], device_id=sibling, device_id_type=MESH_ID
        ).wait_recv()
        x = qb[pl.ds(a * 4, 4)].reshape(ROWS, 128)
        zero = jnp.zeros((ROWS, 64), bf16)
        qs[a, 0:ROWS] = jnp.concatenate([x[:, :64], zero], axis=1)
        qs[a, ROWS:QT] = jnp.concatenate([x[:, 64:], zero], axis=1)

    queries(0, 1)

    def stage(na, nb, sa, sb, ala, alb, mna, mnb):
        if na is not None:
            a, c, _ = na
            q = qs[a]
            m_old = m_ref[a]
            mx = None
        if nb is not None:
            a2, _, vslot = nb
            m_b = mnb[...]
            o = None
        for j in range(BLOCK // KC):
            ks = slice(j * KC, (j + 1) * KC)
            if na is not None:
                s = lax.dot_general(
                    q,
                    kvb[j // 2, pl.ds(c * 4 + 2 * (j % 2), 2)].reshape(KC, 128),
                    (((1,), (1,)), ((), ())),
                    preferred_element_type=f32,
                )
                sa[:, ks] = s
                for l in range(KC // 128):
                    t = s[:, l * 128:(l + 1) * 128]
                    mx = t if mx is None else jnp.maximum(mx, t)
            if nb is not None:
                ps = []
                for l in range(KC // 128):
                    at = j * KC + l * 128
                    ps.append(jnp.exp2((sb[:, at:at + 128] - m_b) * SCALE).astype(bf16))
                p = jnp.concatenate(ps, axis=1)
                part = jnp.dot(p, va[vslot, ks], preferred_element_type=f32)
                o = part if o is None else o + part
        if nb is not None:
            acc[a2] = acc[a2] * alb[...] + o
        if na is not None:
            m_new = jnp.maximum(m_old, jnp.max(mx, axis=1, keepdims=True))
            m_ref[a] = m_new
            mna[...] = m_new
            ala[...] = jnp.exp2((m_old - m_new) * SCALE)

    def finish(a, last):
        @pl.when(last)
        def _():
            y = acc[a]
            total = jnp.concatenate([y[:ROWS, :64], y[ROWS:, :64]], axis=1)
            z = jnp.concatenate([y[:ROWS, 64:], y[ROWS:, 64:]], axis=1)
            z = (z / total).astype(bf16)
            osend[pl.ds(a * 4, 4)] = z.reshape(4, PART, 128)
            b3 = lax.div(a, 8)
            b2 = lax.div(a, 4) - 2 * b3
            b1 = lax.div(a, 2) - 4 * b3 - 2 * b2
            b0 = a - 8 * b3 - 4 * b2 - 2 * b1
            high = b3 * flip[0] + b2 * flip[1] + b1 * flip[2]
            for w in range(4):
                low = b0 * flip[3] + (w // 2) * flip[4] + (w % 2) * flip[5]

                def send():
                    pltpu.make_async_remote_copy(
                        osend.at[a * 4 + w], obuf.at[chip], o_send, o_recv,
                        device_id=(blk + lax.div(high, 8), head + 2 * low), device_id_type=MESH_ID,
                    ).start()

                if w:
                    send()
                else:
                    pl.when(a > 0)(send)

                    @pl.when(a == 0)
                    def _():
                        own = pltpu.make_async_copy(osend.at[0], obuf.at[chip], loc.at[2])
                        own.start()
                        own.wait()

    even, odd = (s0, al0, mn0), (s1, al1, mn1)

    def step(na, nb, turn):
        x, y = (odd, even) if turn else (even, odd)
        stage(na, nb, x[0], y[0], x[1], y[1], x[2], y[2])

    ready(0, 0)
    queries(1)
    step((1, 0, 0), None, 0)

    def two_blocks(b3, b2, b1):
        h = 4 * b3 + 2 * b2 + b1
        more = h < NBLK // 2 - 1
        pairs, lasts, news = [], [], []
        for b0 in range(2):
            c = 2 * h + b0
            ones = [b3 * b2 * b1 * b0, b3 * b2 * b1, b3 * b2, b3, b3 * b2 * b1 * b0]
            fresh = [b3 + b2 + b1 == 0, b3 + b2 + b1 == 0, b3 + b2 == 0, b3 == 0]
            near = [1 - 2 * b0, 2 - 4 * b1, 4 - 8 * b2, 8 - 16 * b3, 0]
            for i in range(5):
                pairs.append((c + near[i], c, b0))
                news.append(fresh[i] if i < 4 and not (b0 and i == 0) else None)
                lasts.append(None if i in (0, 4) and b0 == 0 else ones[i] == 1)
        for k in range(10):
            if k in (0, 2, 4, 6):

                @pl.when(h < (4 if k < 4 else 3))
                def _():
                    send_kv(4 * h + 2 + k // 2)

            later_q = {1: (6, 10), 3: (7, 11), 5: (12, 13), 7: (14, 15)}.get(k, ())
            if later_q:

                @pl.when(h == 0)
                def _():
                    for r in later_q:
                        send_q(r)

            if k == 1:
                arrive(2 * h + 1)
            if k == 4:
                ready(2 * h + 1, 1)
            if k == 6:

                @pl.when(more)
                def _():
                    arrive(2 * h + 2)

            turn = (k + 1) % 2
            if k < 9:
                if news[k + 1] is not None:
                    pl.when(news[k + 1])(lambda: queries(pairs[k + 1][0]))
                step(pairs[k + 1], pairs[k], turn)
            else:

                @pl.when(more)
                def _():
                    ready(2 * h + 2, 0)
                    step((2 * h + 3, 2 * h + 2, 0), pairs[9], turn)

                @pl.when(jnp.logical_not(more))
                def _():
                    step(None, pairs[9], turn)

            if lasts[k] is not None:
                finish(pairs[k][0], lasts[k])

    over_bits(3, two_blocks)

    def done(ref, sem):
        return pltpu.make_async_remote_copy(
            ref, ref, sem, sem, device_id=sibling, device_id_type=MESH_ID
        )

    done(obuf.at[pl.ds(0, CHIPS - 1)], o_recv).wait_recv()

    @pl.loop(0, HEADS // 2)
    def _(g):
        cols = pl.ds(pl.multiple_of(g * 128, 128), 128)
        for c in range(2):
            e = obuf[g * 4 + c]
            o = obuf[g * 4 + 2 + c]
            out_ref[c * 128:c * 128 + 64, cols] = jnp.concatenate([e[:, :64], o[:, :64]], axis=1)
            out_ref[c * 128 + 64:c * 128 + 128, cols] = jnp.concatenate(
                [e[:, 64:], o[:, 64:]], axis=1
            )

    done(osend.at[pl.ds(0, CHIPS - 1)], o_send).wait_send()
    done(qb.at[pl.ds(0, CHIPS - 1)], q_send).wait_send()
    done(kvb.at[0, pl.ds(0, CHIPS - 1)], kv_send).wait_send()
    done(kvb.at[0], f_send).wait_send()


def on_device(qkv):
    vmem = pltpu.VMEM
    bf16, f32 = jnp.bfloat16, jnp.float32
    dma = pltpu.SemaphoreType.DMA
    return pl.pallas_call(
        kernel,
        name="butterfly",
        out_shape=jax.ShapeDtypeStruct((ROWS, D), bf16),
        in_specs=[pl.BlockSpec(memory_space=pl.ANY)],
        out_specs=pl.BlockSpec(memory_space=vmem),
        scratch_shapes=[
            vmem((ROWS, 3 * D), bf16),
            vmem((CHIPS, PART, 128), bf16),
            vmem((HEADS, ROWS, 128), bf16),
            vmem((CHIPS, PART, 128), bf16),
            vmem((2, CHIPS, ROWS, 128), bf16),
            vmem((NBLK, QT, 128), bf16),
            vmem((2, BLOCK, 128), bf16),
            vmem((NBLK, QT, 128), f32),
            vmem((NBLK, QT, 128), f32),
            vmem((QT, BLOCK), f32),
            vmem((QT, BLOCK), f32),
            vmem((QT, 128), f32),
            vmem((QT, 128), f32),
            vmem((QT, 128), f32),
            vmem((QT, 128), f32),
            vmem((CHIPS, PART, 128), bf16),
            vmem((CHIPS, PART, 128), bf16),
            dma, dma((NBLK,)), dma, dma((NBLK,)), dma, dma((NBLK,)), dma, dma, dma((4,)),
        ],
        compiler_params=pltpu.CompilerParams(
            collective_id=0, has_side_effects=True, vmem_limit_bytes=60 * 2**20
        ),
    )(qkv)


def solution(mesh):
    spec = P(("blk", "head"), None)
    return jax.shard_map(
        on_device, mesh=mesh, in_specs=(spec,), out_specs=spec, check_vma=False
    )
```

```python
import math

import jax
import jax.numpy as jnp
from jax import lax
from jax.experimental import pallas as pl
from jax.experimental.pallas import tpu as pltpu
from jax.sharding import PartitionSpec as P

HEAD_DIM = 64
BLOCK = 2048
NBLK = 16
HEADS = 32
D = HEADS * HEAD_DIM
CHIPS = 64
ROWS = 256
PART = 64
QT = 512
KC = 512
PAIRS = 5 * NBLK
SCALE = HEAD_DIM**-0.5 * math.log2(math.e)
MESH_ID = pl.DeviceIdType.MESH


def over_bits(count, body):
    def level(bits):
        if len(bits) == count:
            body(*bits)
            return

        @pl.loop(0, 2)
        def _(b):
            level(bits + (b,))

    level(())


def kernel(
    x_ref, out_ref,
    sendq, sendkv, qb, kvb, qs, va, m_ref, acc, s0, s1, al0, al1, mn0, mn1, osend, obuf,
    q_send, q_recv, kv_send, kv_recv, f_send, f_recv, o_send, o_recv, loc,
):
    blk = lax.axis_index("blk")
    head = lax.axis_index("head")
    chip = blk * 8 + lax.div(head, 2)
    core = lax.rem(head, 2)
    f32, bf16 = jnp.float32, jnp.bfloat16

    flip = []
    for i in range(6):
        w = 32 >> i
        flip.append(w * (1 - 2 * lax.rem(lax.div(chip, w), 2)))
    sibling = (blk, head + 1 - 2 * core)

    def every_chip(body):
        def four(b5, b4, b3, b2):
            r = 8 * b5 + 4 * b4 + 2 * b3 + b2
            high = b5 * flip[0] + b4 * flip[1] + b3 * flip[2]
            to_blk = blk + lax.div(high, 8)
            for w in range(4):
                mid = b2 * flip[3] + (w // 2) * flip[4]
                low = mid + (w % 2) * flip[5]
                to = chip + high + low
                owned = half + lax.div(high + mid, 2)
                device = (to_blk, head + 2 * low)
                if w:
                    body(r * 4 + w, to, owned, device)
                else:

                    @pl.when(r > 0)
                    def _():
                        body(r * 4, to, owned, device)

        over_bits(4, four)

    half = lax.div(chip, 2)
    barrier = pltpu.get_barrier_semaphore()

    @every_chip
    def _(t, to, owned, device):
        pl.semaphore_signal(barrier, inc=1, device_id=device, device_id_type=MESH_ID)

    pl.semaphore_signal(barrier, inc=1, device_id=sibling, device_id_type=MESH_ID)

    @pl.loop(0, HEADS // 2)
    def _(g):
        x = x_ref[:, pl.ds(pl.multiple_of(g * 128, 128), 128)]
        for e in range(2):
            y = x[:, e * 64:(e + 1) * 64]
            for c in range(2):
                sendq[g * 4 + e * 2 + c] = jnp.concatenate(
                    [y[c * 128:c * 128 + 64], y[c * 128 + 64:c * 128 + 128]], axis=1
                )

    @pl.loop(0, HEADS // 2)
    def _(g):
        k = x_ref[:, pl.ds(pl.multiple_of(D + g * 128, 128), 128)]
        v = x_ref[:, pl.ds(pl.multiple_of(2 * D + g * 128, 128), 128)]
        for e in range(2):
            h = slice(e * 64, (e + 1) * 64)
            sendkv[g * 2 + e] = jnp.concatenate([k[:, h], v[:, h]], axis=1)

    pl.semaphore_wait(barrier, CHIPS)

    def place(b3, b2, b1, b0, w):
        high = b3 * flip[0] + b2 * flip[1] + b1 * flip[2]
        mid = b0 * flip[3] + (w // 2) * flip[4]
        low = mid + (w % 2) * flip[5]
        return chip + high + low, half + lax.div(high + mid, 2), (blk + lax.div(high, 8), head + 2 * low)

    def bits_of(r):
        return [lax.div(r, 8 >> i) - 2 * lax.div(r, 16 >> i) for i in range(4)]

    def send_q(r):
        static = isinstance(r, int)
        bits = [(r >> (3 - i)) & 1 for i in range(4)] if static else bits_of(r)
        for w in range(4):
            if static and r == 0 and w == 0:
                continue
            to, _, device = place(*bits, w)
            pltpu.make_async_remote_copy(
                sendq.at[to], qb.at[r * 4 + w], q_send, q_recv.at[r],
                device_id=device, device_id_type=MESH_ID,
            ).start()

    def send_kv(r):
        static = isinstance(r, int)
        bits = [(r >> (3 - i)) & 1 for i in range(4)] if static else bits_of(r)
        for w in range(4):
            if static and r == 0 and w == 0:
                continue
            _, owned, device = place(*bits, w)
            pltpu.make_async_remote_copy(
                sendkv.at[owned], kvb.at[core, r * 4 + w], kv_send, kv_recv.at[r],
                device_id=device, device_id_type=MESH_ID,
            ).start()

    send_q(0)

    @pl.loop(0, 4)
    def _(u):
        square = lax.div(u * (u - 1), 2)
        send_q(1 + u + square + lax.div(square * (u - 2), 3))

    send_kv(0)

    @pl.loop(0, 3)
    def _(u):
        send_q(3 + 2 * u + u * (u - 1))

    send_kv(1)

    own_q = pltpu.make_async_copy(sendq.at[chip], qb.at[0], loc.at[0])
    own_kv = pltpu.make_async_copy(sendkv.at[half], kvb.at[core, 0], loc.at[1])
    own_q.start()
    own_kv.start()

    def forward(c):
        rows = pl.ds(c * 4, 4)
        return pltpu.make_async_remote_copy(
            kvb.at[core, rows], kvb.at[core, rows], f_send, f_recv.at[c],
            device_id=sibling, device_id_type=MESH_ID,
        )

    def landed(c, skip):
        part = kvb.at[core, pl.ds(c * 4 + skip, 4 - skip)]
        pltpu.make_async_remote_copy(
            part, part, kv_send, kv_recv.at[c], device_id=sibling, device_id_type=MESH_ID
        ).wait_recv()

    def arrive(c):
        landed(c, 0)
        forward(c).start()

    def ready(c, slot):
        part = kvb.at[1 - core, pl.ds(c * 4, 4)]
        pltpu.make_async_remote_copy(
            part, part, f_send, f_recv.at[c], device_id=sibling, device_id_type=MESH_ID
        ).wait_recv()
        low = lax.broadcasted_iota(jnp.int32, (ROWS, 128), 1) < 64

        @pl.loop(0, 2)
        def _(z):
            for w in range(4):
                t = kvb[z, c * 4 + w]
                rows = pl.ds(pl.multiple_of((z * 4 + w) * ROWS, ROWS), ROWS)
                va[slot, rows] = jnp.where(low, jnp.ones_like(t), t)

    own_kv.wait()
    landed(0, 1)
    forward(0).start()

    m_ref[...] = jnp.full_like(m_ref, -jnp.inf)
    acc[...] = jnp.zeros_like(acc)

    own_q.wait()
    def queries(a, own=0):
        got = qb.at[pl.ds(a * 4 + own, 4 - own)]
        pltpu.make_async_remote_copy(
            got, got, q_send, q_recv.at[a], device_id=sibling, device_id_type=MESH_ID
        ).wait_recv()
        x = qb[pl.ds(a * 4, 4)].reshape(ROWS, 128)
        zero = jnp.zeros((ROWS, 64), bf16)
        qs[a, 0:ROWS] = jnp.concatenate([x[:, :64], zero], axis=1)
        qs[a, ROWS:QT] = jnp.concatenate([x[:, 64:], zero], axis=1)

    queries(0, 1)

    def stage(na, nb, sa, sb, ala, alb, mna, mnb):
        if na is not None:
            a, c, _ = na
            q = qs[a]
            m_old = m_ref[a]
            mx = None
        if nb is not None:
            a2, _, vslot = nb
            m_b = mnb[...]
            o = None
        for j in range(BLOCK // KC):
            ks = slice(j * KC, (j + 1) * KC)
            if na is not None:
                s = lax.dot_general(
                    q,
                    kvb[j // 2, pl.ds(c * 4 + 2 * (j % 2), 2)].reshape(KC, 128),
                    (((1,), (1,)), ((), ())),
                    preferred_element_type=f32,
                )
                sa[:, ks] = s
                for l in range(KC // 128):
                    t = s[:, l * 128:(l + 1) * 128]
                    mx = t if mx is None else jnp.maximum(mx, t)
            if nb is not None:
                ps = []
                for l in range(KC // 128):
                    at = j * KC + l * 128
                    ps.append(jnp.exp2((sb[:, at:at + 128] - m_b) * SCALE).astype(bf16))
                p = jnp.concatenate(ps, axis=1)
                part = jnp.dot(p, va[vslot, ks], preferred_element_type=f32)
                o = part if o is None else o + part
        if nb is not None:
            acc[a2] = acc[a2] * alb[...] + o
        if na is not None:
            m_new = jnp.maximum(m_old, jnp.max(mx, axis=1, keepdims=True))
            m_ref[a] = m_new
            mna[...] = m_new
            ala[...] = jnp.exp2((m_old - m_new) * SCALE)

    def finish(a, last):
        @pl.when(last)
        def _():
            y = acc[a]
            total = jnp.concatenate([y[:ROWS, :64], y[ROWS:, :64]], axis=1)
            z = jnp.concatenate([y[:ROWS, 64:], y[ROWS:, 64:]], axis=1)
            z = (z / total).astype(bf16)
            osend[pl.ds(a * 4, 4)] = z.reshape(4, PART, 128)
            b3 = lax.div(a, 8)
            b2 = lax.div(a, 4) - 2 * b3
            b1 = lax.div(a, 2) - 4 * b3 - 2 * b2
            b0 = a - 8 * b3 - 4 * b2 - 2 * b1
            high = b3 * flip[0] + b2 * flip[1] + b1 * flip[2]
            for w in range(4):
                low = b0 * flip[3] + (w // 2) * flip[4] + (w % 2) * flip[5]

                def send():
                    pltpu.make_async_remote_copy(
                        osend.at[a * 4 + w], obuf.at[chip], o_send, o_recv,
                        device_id=(blk + lax.div(high, 8), head + 2 * low), device_id_type=MESH_ID,
                    ).start()

                if w:
                    send()
                else:
                    pl.when(a > 0)(send)

                    @pl.when(a == 0)
                    def _():
                        own = pltpu.make_async_copy(osend.at[0], obuf.at[chip], loc.at[2])
                        own.start()
                        own.wait()

    even, odd = (s0, al0, mn0), (s1, al1, mn1)

    def step(na, nb, turn):
        x, y = (odd, even) if turn else (even, odd)
        stage(na, nb, x[0], y[0], x[1], y[1], x[2], y[2])

    ready(0, 0)
    queries(1)
    step((1, 0, 0), None, 0)

    def two_blocks(b3, b2, b1):
        h = 4 * b3 + 2 * b2 + b1
        more = h < NBLK // 2 - 1
        pairs, lasts, news = [], [], []
        for b0 in range(2):
            c = 2 * h + b0
            ones = [b3 * b2 * b1 * b0, b3 * b2 * b1, b3 * b2, b3, b3 * b2 * b1 * b0]
            fresh = [b3 + b2 + b1 == 0, b3 + b2 + b1 == 0, b3 + b2 == 0, b3 == 0]
            near = [1 - 2 * b0, 2 - 4 * b1, 4 - 8 * b2, 8 - 16 * b3, 0]
            for i in range(5):
                pairs.append((c + near[i], c, b0))
                news.append(fresh[i] if i < 4 and not (b0 and i == 0) else None)
                lasts.append(None if i in (0, 4) and b0 == 0 else ones[i] == 1)
        for k in range(10):
            if k in (0, 2, 4, 6):

                @pl.when(h < (4 if k < 4 else 3))
                def _():
                    send_kv(4 * h + 2 + k // 2)

            later_q = {1: (6, 4), 3: (7, 4), 5: (12, 1), 7: (14, 1)}.get(k)
            if later_q:

                @pl.when(h == 0)
                def _():
                    @pl.loop(0, 2)
                    def _(u):
                        send_q(later_q[0] + later_q[1] * u)

            if k == 1:
                arrive(2 * h + 1)
            if k == 4:
                ready(2 * h + 1, 1)
            if k == 6:

                @pl.when(more)
                def _():
                    arrive(2 * h + 2)

            turn = (k + 1) % 2
            if k < 9:
                if news[k + 1] is not None:
                    pl.when(news[k + 1])(lambda: queries(pairs[k + 1][0]))
                step(pairs[k + 1], pairs[k], turn)
            else:

                @pl.when(more)
                def _():
                    ready(2 * h + 2, 0)
                    step((2 * h + 3, 2 * h + 2, 0), pairs[9], turn)

                @pl.when(jnp.logical_not(more))
                def _():
                    step(None, pairs[9], turn)

            if lasts[k] is not None:
                finish(pairs[k][0], lasts[k])

    over_bits(3, two_blocks)

    def done(ref, sem):
        return pltpu.make_async_remote_copy(
            ref, ref, sem, sem, device_id=sibling, device_id_type=MESH_ID
        )

    done(obuf.at[pl.ds(0, CHIPS - 1)], o_recv).wait_recv()

    @pl.loop(0, HEADS // 2)
    def _(g):
        cols = pl.ds(pl.multiple_of(g * 128, 128), 128)
        for c in range(2):
            e = obuf[g * 4 + c]
            o = obuf[g * 4 + 2 + c]
            out_ref[c * 128:c * 128 + 64, cols] = jnp.concatenate([e[:, :64], o[:, :64]], axis=1)
            out_ref[c * 128 + 64:c * 128 + 128, cols] = jnp.concatenate(
                [e[:, 64:], o[:, 64:]], axis=1
            )

    done(osend.at[pl.ds(0, CHIPS - 1)], o_send).wait_send()
    done(qb.at[pl.ds(0, CHIPS - 1)], q_send).wait_send()
    done(kvb.at[0, pl.ds(0, CHIPS - 1)], kv_send).wait_send()
    done(kvb.at[0], f_send).wait_send()


def on_device(qkv):
    vmem = pltpu.VMEM
    bf16, f32 = jnp.bfloat16, jnp.float32
    dma = pltpu.SemaphoreType.DMA
    return pl.pallas_call(
        kernel,
        name="butterfly",
        out_shape=jax.ShapeDtypeStruct((ROWS, D), bf16),
        in_specs=[pl.BlockSpec(memory_space=vmem)],
        out_specs=pl.BlockSpec(memory_space=vmem),
        scratch_shapes=[
            vmem((CHIPS, PART, 128), bf16),
            vmem((HEADS, ROWS, 128), bf16),
            vmem((CHIPS, PART, 128), bf16),
            vmem((2, CHIPS, ROWS, 128), bf16),
            vmem((NBLK, QT, 128), bf16),
            vmem((2, BLOCK, 128), bf16),
            vmem((NBLK, QT, 128), f32),
            vmem((NBLK, QT, 128), f32),
            vmem((QT, BLOCK), f32),
            vmem((QT, BLOCK), f32),
            vmem((QT, 128), f32),
            vmem((QT, 128), f32),
            vmem((QT, 128), f32),
            vmem((QT, 128), f32),
            vmem((CHIPS, PART, 128), bf16),
            vmem((CHIPS, PART, 128), bf16),
            dma, dma((NBLK,)), dma, dma((NBLK,)), dma, dma((NBLK,)), dma, dma, dma((3,)),
        ],
        compiler_params=pltpu.CompilerParams(
            collective_id=0, has_side_effects=True, vmem_limit_bytes=60 * 2**20
        ),
    )(qkv)


def solution(mesh):
    spec = P(("blk", "head"), None)
    return jax.shard_map(
        on_device, mesh=mesh, in_specs=(spec,), out_specs=spec, check_vma=False
    )
```
